256 devices in a mesh: dp: 8 (over z), seq: 32 (over x, y, core).
Axes of the slice: x: 4, y: 4, z: 8, core: 2. Of those that a mesh axis runs over, the one named last changes fastest.
Arguments:
- seq_in: bfloat16 [65536, 1536], P(('dp', 'seq')), parts along dimension 0, may hold values from -6 to 6
- conv_gain: float32 [1536], replicated, may hold values from 0.1 to 1.9
- convolution_weight: bfloat16 [3, 1536, 768], replicated, may hold values from -0.09375 to 0.09375
- conv_bias: float32 [768], replicated, may hold values from -3 to 3
- attn_gain: float32 [1536], replicated, may hold values from 0.1 to 1.9
- w_query: bfloat16 [1536, 512], replicated
- w_key: bfloat16 [1536, 128], replicated
- w_value: bfloat16 [1536, 128], replicated, may hold values from -0.15625 to 0.15625
- w_out: bfloat16 [512, 1536], replicated, may hold values from -0.25 to 0.25
Outputs:
- block_out: bfloat16 [65536, 1536], P(('dp', 'seq')), parts along dimension 0
The draws below stay inside these ranges and needn't reach their ends.
There are 8 independent parts, one for each index of `dp`. The reference program is written for one: setup_inputs(seed, part) draws one part's arguments, and reference() takes and returns one part's arrays. A program takes and returns all parts, laid end to end along the dimension named above; an argument that names none is the same for every part. Nothing has to cross between parts.
All inputs are finite; a program needn't handle non-finite values.
Results may differ from the reference program's by a relative error of at most 0.0059.
Values may be sent and summed in bfloat16 or wider, within the bound.
A program may use at most 128 MiB of HBM per device.

```python
import math
import jax
import jax.numpy as jnp
from jax import lax

C = 1536
CO = 768
HEADS = 4
DH = 128
KERNEL_TAPS = 3
DILATION_STEP = 4
SEQUENCE_TOKENS = 8192


def key_matrix(key):
    draw_base = jax.random.normal(jax.random.fold_in(key, 7), (C, DH), jnp.float32)
    return jnp.clip(draw_base, -6.0, 6.0) / math.sqrt(C)


def draw_w_key(key, part):
    return key_matrix(key).astype(jnp.bfloat16)


def draw_w_query(key, part):
    draw_base = jax.random.normal(jax.random.fold_in(key, 13), (C, HEADS * DH), jnp.float32)
    draw_base = jnp.clip(draw_base, -4.0, 4.0) * (3.0 / math.sqrt(C))
    return draw_base.astype(jnp.bfloat16)


def steps_of(stream_key, shape, split, low, top_value):
    def one(axis_at, shards_of):
        heights = jax.random.uniform(jax.random.fold_in(jax.random.fold_in(stream_key, 6), axis_at), (shards_of,), jnp.float32, low / len(split), top_value / len(split))
        return jnp.repeat(jnp.exp(heights), shape[axis_at] // shards_of).reshape((-1,) + (1,) * (len(shape) - axis_at - 1))

    gain = one(*split[0])
    for cut in split[1:]:
        gain = gain * one(*cut)
    return gain


def bell_draw(key, shape, scale, most, shards=(), dtype=jnp.bfloat16):
    array = scale * jax.random.normal(key, shape, jnp.float32)
    if shards:
        array = array * steps_of(key, shape, shards, -0.22, 0.18)
    return jnp.clip(array, -most, most).astype(dtype)


def setup_inputs(seed: int = 0, part: int = 0) -> dict:
    key_of = jax.random.split(jax.random.key(seed), 10)
    own_keys = jax.random.split(jax.random.fold_in(key_of[9], part), 10)
    seq_in = bell_draw(own_keys[0], (SEQUENCE_TOKENS, C), 1.0, 6.0, ((0, 32),))
    conv_gain = jnp.clip(1.0 + 0.18 * jax.random.normal(key_of[1], (C,), jnp.float32), 0.1, 1.9)
    convolution_weight = bell_draw(key_of[2], (KERNEL_TAPS, C, CO), (KERNEL_TAPS * C) ** -0.5, 0.09375)
    conv_bias = bell_draw(key_of[3], (CO,), 0.5, 3.0, (), jnp.float32)
    attn_gain = jnp.clip(1.0 + 0.18 * jax.random.normal(key_of[4], (C,), jnp.float32), 0.1, 1.9)
    w_query = draw_w_query(jax.random.fold_in(key_of[9], 71), part)
    w_key = draw_w_key(jax.random.fold_in(key_of[9], 71), part)
    w_value = bell_draw(key_of[7], (C, DH), C ** -0.5, 0.15625)
    w_out = bell_draw(key_of[8], (HEADS * DH, C), (HEADS * DH) ** -0.5, 0.25)
    return {"seq_in": seq_in, "conv_gain": conv_gain, "convolution_weight": convolution_weight, "conv_bias": conv_bias, "attn_gain": attn_gain, "w_query": w_query, "w_key": w_key, "w_value": w_value, "w_out": w_out}


def normalize(values, gain_vec):
    wide = values.astype(jnp.float32)
    meansq = lax.optimization_barrier(jnp.mean(wide * wide, axis=-1, keepdims=True))
    return wide * lax.rsqrt(meansq + 1e-06) * gain_vec

def reference(seq_in, conv_gain, convolution_weight, conv_bias, attn_gain, w_query, w_key, w_value, w_out):
    receptive_reach = DILATION_STEP * (KERNEL_TAPS - 1) // 2
    normed = normalize(seq_in, conv_gain).astype(jnp.bfloat16)
    padded_tokens = jnp.pad(normed, ((receptive_reach, receptive_reach), (0, 0)))
    convolved_total = jnp.zeros((SEQUENCE_TOKENS, CO), jnp.float32)
    for tap_index in range(KERNEL_TAPS):
        convolved_total = convolved_total + jnp.dot(padded_tokens[tap_index * DILATION_STEP:tap_index * DILATION_STEP + SEQUENCE_TOKENS], convolution_weight[tap_index], preferred_element_type=jnp.float32)
    activated = jax.nn.gelu(convolved_total + conv_bias, approximate=True)
    wide_in = seq_in.astype(jnp.float32)
    hidden = jnp.concatenate([wide_in[:, :CO] + activated, wide_in[:, CO:]], axis=1).astype(jnp.bfloat16)
    attn_in = normalize(hidden, attn_gain).astype(jnp.bfloat16)
    queries = jnp.dot(attn_in, w_query, preferred_element_type=jnp.float32).astype(jnp.bfloat16)
    keys = jnp.dot(attn_in, w_key, preferred_element_type=jnp.float32).astype(jnp.bfloat16)
    values = jnp.dot(attn_in, w_value, preferred_element_type=jnp.float32).astype(jnp.bfloat16)
    key_wide = keys.astype(jnp.float32)
    value_wide = values.astype(jnp.float32)
    block_len = math.gcd(SEQUENCE_TOKENS, 512)
    query_blocks = queries.reshape(SEQUENCE_TOKENS // block_len, block_len, HEADS, DH)

    def attend(query_block):
        scores = jnp.einsum('thd,kd->htk', query_block.astype(jnp.float32), key_wide) * DH ** (-0.5)
        top_score = lax.optimization_barrier(jnp.max(scores, axis=-1, keepdims=True))
        expd = jnp.exp(scores - top_score)
        totals = lax.optimization_barrier(jnp.sum(expd, axis=-1))
        weights = expd.astype(jnp.bfloat16).astype(jnp.float32)
        summed = jnp.einsum('htk,kd->htd', weights, value_wide)
        result = summed / totals[..., None]
        return jnp.transpose(result, (1, 0, 2)).reshape(block_len, HEADS * DH)
    attended = lax.map(attend, query_blocks).reshape(SEQUENCE_TOKENS, HEADS * DH).astype(jnp.bfloat16)
    mixed = hidden.astype(jnp.float32) + jnp.dot(attended, w_out, preferred_element_type=jnp.float32)
    return mixed.astype(jnp.bfloat16)
```

```python
import jax
import jax.numpy as jnp
from jax import lax
from jax.experimental import pallas as pl
from jax.experimental.pallas import tpu as pltpu
from jax.sharding import PartitionSpec as P

ROWS = 256
C = 1536
CO = 768
HEADS = 4
DH = 128
REACH = 4
SIDE = 4
SCALE = 1.4426950408889634 / (DH**0.5)
BF = jnp.bfloat16
F32 = jnp.float32

CHUNKS = (
    ((0, 0, 0), (1, 0, 0),),
    ((0, 1, 0), (0, 3, 0), (0, 0, 1), (0, 0, 3),),
    ((1, 1, 0), (1, 3, 0), (1, 0, 1), (1, 0, 3),),
    ((0, 2, 0), (0, 0, 2), (1, 2, 0), (1, 0, 2),),
    ((0, 1, 1), (0, 1, 3), (0, 3, 1), (0, 3, 3),),
    ((1, 1, 1), (1, 1, 3), (1, 3, 1), (1, 3, 3),),
    ((0, 2, 1), (0, 2, 3), (0, 1, 2), (0, 3, 2),),
    ((1, 2, 1), (1, 2, 3), (1, 1, 2), (1, 3, 2),),
    ((0, 2, 2), (1, 2, 2),),
)
ACTS = {
    (0, 0): ((1, 0, 0, 0), (1, 0, 0, 1),),
    (0, 3): ((0, 1, 0, 0), (0, 3, 0, 0), (0, 0, 1, 0), (0, 0, 3, 0),),
    (1, 0): ((0, 1, 0, 1), (0, 3, 0, 1), (0, 0, 1, 1), (0, 0, 3, 1),),
    (1, 3): ((0, 2, 0, 0), (0, 1, 3, 0), (1, 1, 0, 0), (1, 3, 0, 0), (1, 0, 1, 0), (1, 0, 3, 0),),
    (2, 0): ((1, 1, 0, 1), (1, 3, 0, 1), (1, 0, 1, 1), (1, 0, 3, 1),),
    (2, 1): ((0, 1, 1, 0), (0, 3, 3, 0),),
    (2, 3): ((0, 3, 1, 0), (0, 1, 3, 1), (1, 2, 0, 0), (0, 0, 2, 0), (0, 2, 0, 1), (0, 1, 1, 1), (0, 3, 3, 1), (1, 0, 2, 0),),
    (3, 0): ((0, 3, 1, 1), (0, 0, 2, 1), (1, 2, 0, 1), (0, 2, 1, 0), (0, 2, 3, 0), (1, 0, 2, 1),),
    (3, 1): ((0, 1, 2, 0), (0, 1, 2, 1),),
    (3, 3): ((0, 3, 2, 0), (0, 2, 3, 1),),
    (4, 1): ((0, 2, 1, 1), (0, 3, 2, 1),),
    (4, 3): ((1, 1, 3, 0), (1, 1, 1, 0), (1, 3, 3, 0), (1, 3, 1, 0),),
    (5, 0): ((0, 2, 2, 0), (1, 1, 3, 1), (1, 1, 1, 1), (1, 3, 3, 1), (1, 3, 1, 1),),
    (5, 3): ((0, 2, 2, 1),),
    (6, 3): ((1, 2, 1, 0), (1, 2, 3, 0), (1, 1, 2, 0), (1, 3, 2, 0),),
    (7, 0): ((1, 1, 2, 1), (1, 2, 3, 1), (1, 2, 1, 1), (1, 3, 2, 1),),
    (7, 3): ((1, 2, 2, 0),),
    (8, 0): ((1, 2, 2, 1),),
}


ORDER = tuple(b for ch in CHUNKS for b in ch)
SLOT = {b: i for i, b in enumerate(ORDER)}


def nt_dot(a, b):
    return lax.dot_general(a, b, (((1,), (1,)), ((), ())), preferred_element_type=F32)


def nn_dot(a, b):
    return jnp.dot(a, b, preferred_element_type=F32)


def kernel(
    x_hbm, cg_hbm, cw_hbm, cb_hbm, ag_hbm, wq_hbm, wk_hbm, wv_hbm, wo_hbm,
    out_ref,
    x_ref, cg_ref, cw_ref, cb_ref, ag_ref, wq_ref, wkv_ref, wo_ref,
    edge_ref, ext_ref, hid_ref, ain_ref, q_ref, k_ref, v_ref,
    s_ref, acc_ref, stat_ref, att_ref,
    lsem, hsend, hrecv, ssem, rsem,
):
    dp = lax.axis_index("dp")
    me = lax.axis_index("seq")
    core = lax.rem(me, 2)
    chip = me // 2
    cx = chip // SIDE
    cy = lax.rem(chip, SIDE)

    def at(ix, iy, co):
        return (lax.rem(ix, SIDE) * SIDE + lax.rem(iy, SIDE)) * 2 + co

    da_x = 1 - core
    da_y = core
    a_up = at(cx + da_x, cy + da_y, core)
    a_dn = at(cx + da_x * 3, cy + da_y * 3, core)
    b_up = at(cx + da_y, cy + da_x, core)
    b_dn = at(cx + da_y * 3, cy + da_x * 3, core)
    mate = chip * 2 + (1 - core)
    nxt = lax.rem(me + 1, 32)
    prv = lax.rem(me + 31, 32)
    MESH = pl.DeviceIdType.MESH

    def load(src, dst, i):
        return pltpu.make_async_copy(src, dst, lsem.at[i])

    loads = [
        load(x_hbm, x_ref, 0),
        load(cg_hbm, cg_ref, 1),
        load(cw_hbm.at[1], cw_ref.at[1], 2),
        load(cw_hbm.at[0], cw_ref.at[0], 3),
        load(cw_hbm.at[2], cw_ref.at[2], 4),
        load(cb_hbm, cb_ref, 5),
        load(ag_hbm, ag_ref, 6),
        load(wk_hbm, wkv_ref.at[:, 0:DH], 7),
        load(wv_hbm, wkv_ref.at[:, DH : 2 * DH], 8),
        load(wq_hbm, wq_ref, 9),
        load(wo_hbm, wo_ref, 10),
    ]
    for cp in loads:
        cp.start()

    barrier = pltpu.get_barrier_semaphore()
    for who in (nxt, prv, a_up, a_dn, b_up, b_dn, mate):
        pl.semaphore_signal(barrier, inc=1, device_id=(dp, who), device_id_type=MESH)
    pl.semaphore_wait(barrier, 7)

    def remote(src, dst, ss, rs, who):
        return pltpu.make_async_remote_copy(
            src_ref=src, dst_ref=dst, send_sem=ss, recv_sem=rs,
            device_id=(dp, who), device_id_type=MESH,
        )

    halo = [
        remote(x_hbm.at[pl.ds(0, 8)], edge_ref.at[0], hsend.at[0], hrecv.at[0], prv),
        remote(x_hbm.at[pl.ds(ROWS - 8, 8)], edge_ref.at[1], hsend.at[1], hrecv.at[1], nxt),
    ]
    for cp in halo:
        cp.start()

    def norm_rows(wide, gain):
        ms = jnp.sum(wide * wide, axis=-1, keepdims=True) * (1.0 / C)
        return wide * lax.rsqrt(ms + 1e-06) * gain

    loads[0].wait()
    loads[1].wait()
    cgain = cg_ref[...].reshape(1, C)
    for i in range(0, ROWS, 32):
        ext_ref[i : i + 32, :] = norm_rows(x_ref[i : i + 32, :].astype(F32), cgain).astype(BF)

    loads[2].wait()
    for n in range(3):
        cols = slice(n * 256, (n + 1) * 256)
        acc_ref[:, cols] = nn_dot(ext_ref[0:ROWS, :], cw_ref[1, :, cols])

    for cp in halo:
        cp.wait_recv()
    last_ok = jnp.where(me < 31, 1.0, 0.0).astype(F32)
    first_ok = jnp.where(me > 0, 1.0, 0.0).astype(F32)
    edge = jnp.concatenate(
        [edge_ref[0].astype(F32) * last_ok, edge_ref[1].astype(F32) * first_ok], axis=0
    )
    ext_ref[ROWS : ROWS + 16, :] = norm_rows(edge, cgain).astype(BF)

    loads[3].wait()
    loads[4].wait()
    loads[5].wait()
    cbias = cb_ref[...].reshape(1, CO)
    for n in range(3):
        cols = slice(n * 256, (n + 1) * 256)
        up = nn_dot(ext_ref[...], cw_ref[0, :, cols])
        dn = nn_dot(ext_ref[...], cw_ref[2, :, cols])
        up = pltpu.roll(up, REACH, 0)[0:ROWS]
        dn = pltpu.roll(dn, ROWS + 16 - REACH, 0)[0:ROWS]
        z = up + acc_ref[:, cols] + dn + cbias[:, cols]
        g = jax.nn.gelu(z, approximate=True)
        hid_ref[:, cols] = (x_ref[:, cols].astype(F32) + g).astype(BF)

    loads[6].wait()
    again = ag_ref[...].reshape(1, C)
    for i in range(0, ROWS, 32):
        wide = jnp.concatenate([hid_ref[i : i + 32, :], x_ref[i : i + 32, CO:]], axis=1).astype(F32)
        ain_ref[i : i + 32, :] = norm_rows(wide, again).astype(BF)

    loads[7].wait()
    loads[8].wait()
    kv = nn_dot(ain_ref[...], wkv_ref[...])
    k_ref[0] = kv[:, 0:DH].astype(BF)
    v_ref[0] = kv[:, DH : 2 * DH].T.astype(BF)

    sends = []

    def push(part, src, kind, da, db, who):
        ref = v_ref if part else k_ref
        i = len(sends)
        dst = SLOT[(kind, da, db)]
        cp = remote(ref.at[src], ref.at[dst], ssem.at[i], rsem.at[part, dst], who)
        cp.start()
        sends.append(cp)

    def forward(kind, da, db, part):
        if kind:
            return
        src = SLOT[(kind, da, db)]
        if da == 0 and db == 0:
            push(part, src, 0, 1, 0, a_up)
            push(part, src, 0, 3, 0, a_dn)
        if (da, db, part) == (1, 0, 0):
            push(part, src, 0, 2, 0, a_up)
        if (da, db, part) == (3, 0, 1):
            push(part, src, 0, 2, 0, a_dn)
        if db == 0:
            push(part, src, 0, da, 1, b_up)
            push(part, src, 0, da, 3, b_dn)
        if db == 1 and part == 0:
            push(part, src, 0, da, 2, b_up)
        if db == 3 and part == 1:
            push(part, src, 0, da, 2, b_dn)
        push(part, src, 1, da, db, mate)

    def arrive(kind, da, db, part):
        dst = SLOT[(kind, da, db)]
        ref = v_ref if part else k_ref
        remote(ref.at[dst], ref.at[dst], ssem.at[0], rsem.at[part, dst], mate).wait_recv()

    def act(key):
        for msg in ACTS.get(key, ()):
            arrive(*msg)
            forward(*msg)

    forward(0, 0, 0, 0)
    forward(0, 0, 0, 1)

    loads[9].wait()
    qa = nn_dot(ain_ref[...], wq_ref[...]) * SCALE
    for h in range(HEADS):
        q_ref[h * ROWS : (h + 1) * ROWS, :] = qa[:, h * DH : (h + 1) * DH].astype(BF)

    def fold8(x, op):
        return op(x.reshape(x.shape[0] // 8, 8, x.shape[1]), axis=0)

    def scores(slot, r, buf, j):
        s = nt_dot(k_ref[slot], q_ref[r * ROWS : (r + 1) * ROWS, :])
        s_ref[buf, j * 256 : (j + 1) * 256, :] = s
        return fold8(s, jnp.max)

    stat_ref[0:8, :] = jnp.full((8, HEADS * ROWS), -jnp.inf, F32)
    stat_ref[8:16, :] = jnp.zeros((8, HEADS * ROWS), F32)
    acc_ref[0:DH, :] = jnp.zeros((DH, HEADS * ROWS), F32)
    act((0, 0))
    slots = [SLOT[b] for b in CHUNKS[0]]
    top = None
    for j, sl in enumerate(slots):
        t = scores(sl, 0, 0, j)
        top = t if top is None else jnp.maximum(top, t)
    for i in range(len(CHUNKS)):
        slots = [SLOT[b] for b in CHUNKS[i]]
        for r in range(HEADS):
            if (i, r) != (0, 0):
                act((i, r))
            if r < HEADS - 1:
                ahead = [(SLOT[b], r + 1) for b in CHUNKS[i]]
            elif i + 1 < len(CHUNKS):
                ahead = [(SLOT[b], 0) for b in CHUNKS[i + 1]]
            else:
                ahead = []
            buf = (i * HEADS + r) % 2
            lanes = slice(r * ROWS, (r + 1) * ROWS)
            m_old = stat_ref[0:1, lanes]
            m_new = jnp.maximum(m_old, jnp.max(top, axis=0, keepdims=True))
            alpha = jnp.exp2(m_old - m_new)
            stat_ref[0:1, lanes] = m_new
            ntop = None
            total = None
            pv = None
            for j in range(max(len(slots), len(ahead))):
                if j < len(ahead):
                    t = scores(ahead[j][0], ahead[j][1], 1 - buf, j)
                    ntop = t if ntop is None else jnp.maximum(ntop, t)
                if j < len(slots):
                    p = jnp.exp2(s_ref[buf, j * 256 : (j + 1) * 256, :] - m_new)
                    y = fold8(p, jnp.sum)
                    total = y if total is None else total + y
                    z = nn_dot(v_ref[slots[j]], p.astype(BF))
                    pv = z if pv is None else pv + z
            stat_ref[8:16, lanes] = stat_ref[8:16, lanes] * alpha + total
            acc_ref[0:DH, lanes] = acc_ref[0:DH, lanes] * alpha + pv
            top = ntop

    for h in range(HEADS):
        lanes = slice(h * ROWS, (h + 1) * ROWS)
        o = acc_ref[0:DH, lanes] / jnp.sum(stat_ref[8:16, lanes], axis=0, keepdims=True)
        att_ref[:, h * DH : (h + 1) * DH] = o.T.astype(BF)
    loads[10].wait()
    for n in range(6):
        cols = slice(n * 256, (n + 1) * 256)
        base = hid_ref[:, cols] if n < 3 else x_ref[:, cols]
        y = base.astype(F32) + nn_dot(att_ref[...], wo_ref[:, cols])
        out_ref[:, cols] = y.astype(BF)

    for cp in halo + sends:
        cp.wait_send()


N_SENDS = 62


def body(x, cg, cw, cb, ag, wq, wk, wv, wo):
    any_spec = pl.BlockSpec(memory_space=pl.ANY)
    return pl.pallas_call(
        kernel,
        out_shape=jax.ShapeDtypeStruct((ROWS, C), BF),
        in_specs=[any_spec] * 9,
        out_specs=pl.BlockSpec(memory_space=pltpu.VMEM),
        scratch_shapes=[
            pltpu.VMEM((ROWS, C), BF),
            pltpu.VMEM((C,), F32),
            pltpu.VMEM((3, C, CO), BF),
            pltpu.VMEM((CO,), F32),
            pltpu.VMEM((C,), F32),
            pltpu.VMEM((C, HEADS * DH), BF),
            pltpu.VMEM((C, 2 * DH), BF),
            pltpu.VMEM((HEADS * DH, C), BF),
            pltpu.VMEM((2, 8, C), BF),
            pltpu.VMEM((ROWS + 16, C), BF),
            pltpu.VMEM((ROWS, CO), BF),
            pltpu.VMEM((ROWS, C), BF),
            pltpu.VMEM((HEADS * ROWS, DH), BF),
            pltpu.VMEM((32, ROWS, DH), BF),
            pltpu.VMEM((32, DH, ROWS), BF),
            pltpu.VMEM((2, 256 * max(len(c) for c in CHUNKS), ROWS), F32),
            pltpu.VMEM((ROWS, HEADS * ROWS), F32),
            pltpu.VMEM((16, HEADS * ROWS), F32),
            pltpu.VMEM((ROWS, HEADS * DH), BF),
            pltpu.SemaphoreType.DMA((11,)),
            pltpu.SemaphoreType.DMA((2,)),
            pltpu.SemaphoreType.DMA((2,)),
            pltpu.SemaphoreType.DMA((N_SENDS,)),
            pltpu.SemaphoreType.DMA((2, 32)),
        ],
        compiler_params=pltpu.CompilerParams(
            collective_id=0, has_side_effects=True, vmem_limit_bytes=60 << 20
        ),
        name="block",
    )(x, cg, cw, cb, ag, wq, wk, wv, wo)


def solution(mesh):
    placed = (P(("dp", "seq"), None), P(), P(), P(), P(), P(), P(), P(), P())
    return jax.shard_map(
        body, mesh=mesh, in_specs=placed, out_specs=P(("dp", "seq"), None), check_vma=False
    )
```

```python
import jax
import jax.numpy as jnp
from jax import lax
from jax.experimental import pallas as pl
from jax.experimental.pallas import tpu as pltpu
from jax.sharding import PartitionSpec as P

ROWS = 256
C = 1536
CO = 768
HEADS = 4
DH = 128
REACH = 4
SIDE = 4
SCALE = 1.4426950408889634 / (DH**0.5)
BF = jnp.bfloat16
F32 = jnp.float32

FAR = (2,)
FAR_A = True
LATE_B = True
CHUNKS = (
    ((0, 0, 0), (1, 0, 0),),
    ((0, 1, 0), (0, 3, 0), (0, 2, 0),),
    ((1, 3, 0), (1, 1, 0), (0, 0, 1),),
    ((0, 0, 3), (1, 2, 0), (1, 0, 3),),
    ((1, 0, 1), (0, 3, 3), (0, 1, 3),),
    ((0, 3, 1), (1, 3, 3), (0, 1, 1),),
    ((0, 2, 3), (1, 3, 1), (1, 1, 3),),
    ((0, 2, 1), (1, 1, 1), (1, 2, 3),),
    ((0, 0, 2), (0, 2, 2), (1, 2, 1),),
    ((1, 0, 2), (0, 1, 2), (0, 3, 2),),
    ((1, 2, 2), (1, 3, 2), (1, 1, 2),),
)
ACTS = {
    (0, 0): ((1, 0, 0, 0), (1, 0, 0, 1),),
    (0, 3): ((0, 1, 0, 0), (0, 3, 0, 0), (0, 2, 0, 0), (0, 0, 1, 0), (0, 0, 3, 0), (0, 3, 0, 1), (0, 1, 0, 1), (0, 2, 0, 1),),
    (1, 3): ((0, 0, 3, 1), (0, 0, 1, 1), (1, 1, 0, 0), (1, 3, 0, 0), (1, 3, 0, 1), (1, 1, 0, 1),),
    (2, 3): ((0, 1, 1, 0), (0, 1, 3, 0), (0, 3, 1, 0), (0, 3, 3, 0), (1, 2, 0, 0), (1, 0, 3, 0), (1, 2, 0, 1), (1, 0, 3, 1),),
    (3, 3): ((0, 2, 1, 0), (0, 2, 3, 0), (1, 0, 1, 0), (1, 0, 1, 1), (0, 2, 2, 0), (0, 0, 2, 0), (0, 3, 3, 1), (0, 3, 1, 1), (0, 1, 3, 1),),
    (4, 3): ((0, 1, 1, 1), (0, 2, 3, 1), (1, 3, 3, 0), (1, 3, 3, 1),),
    (5, 3): ((0, 2, 1, 1), (1, 1, 3, 0), (1, 3, 1, 0), (1, 3, 1, 1), (1, 1, 3, 1),),
    (6, 3): ((0, 0, 2, 1), (0, 2, 2, 1), (0, 1, 2, 0), (0, 3, 2, 1), (1, 1, 1, 0), (1, 2, 3, 0), (1, 1, 1, 1), (1, 2, 3, 1),),
    (7, 3): ((0, 3, 2, 0), (0, 1, 2, 1), (1, 2, 1, 0), (1, 2, 1, 1),),
    (8, 3): ((1, 0, 2, 0), (1, 0, 2, 1),),
    (9, 3): ((1, 2, 2, 0), (1, 2, 2, 1), (1, 1, 2, 0), (1, 3, 2, 1), (1, 3, 2, 0), (1, 1, 2, 1),),
}


ORDER = tuple(b for ch in CHUNKS for b in ch)
SLOT = {b: i for i, b in enumerate(ORDER)}


def nt_dot(a, b):
    return lax.dot_general(a, b, (((1,), (1,)), ((), ())), preferred_element_type=F32)


def nn_dot(a, b):
    return jnp.dot(a, b, preferred_element_type=F32)


def kernel(
    x_hbm, cg_hbm, cw_hbm, cb_hbm, ag_hbm, wq_hbm, wk_hbm, wv_hbm, wo_hbm,
    out_ref,
    x_ref, cg_ref, cw_ref, cb_ref, ag_ref, wq_ref, wkv_ref, wo_ref,
    edge_ref, ext_ref, hid_ref, ain_ref, q_ref, k_ref, v_ref,
    s_ref, acc_ref, stat_ref, att_ref,
    lsem, hsend, hrecv, ssem, rsem,
):
    dp = lax.axis_index("dp")
    me = lax.axis_index("seq")
    core = lax.rem(me, 2)
    chip = me // 2
    cx = chip // SIDE
    cy = lax.rem(chip, SIDE)

    def at(ix, iy, co):
        return (lax.rem(ix, SIDE) * SIDE + lax.rem(iy, SIDE)) * 2 + co

    da_x = 1 - core
    da_y = core
    a_up = at(cx + da_x, cy + da_y, core)
    a_dn = at(cx + da_x * 3, cy + da_y * 3, core)
    b_up = at(cx + da_y, cy + da_x, core)
    b_dn = at(cx + da_y * 3, cy + da_x * 3, core)
    a_far = at(cx + da_x * 2, cy + da_y * 2, core)
    b_far = at(cx + da_y * 2, cy + da_x * 2, core)
    mate = chip * 2 + (1 - core)
    nxt = lax.rem(me + 1, 32)
    prv = lax.rem(me + 31, 32)
    MESH = pl.DeviceIdType.MESH

    def load(src, dst, i):
        return pltpu.make_async_copy(src, dst, lsem.at[i])

    def wcols(n):
        return slice(n * 256, (n + 1) * 256)

    loads = [
        load(x_hbm, x_ref, 0),
        load(cg_hbm, cg_ref, 1),
        load(cw_hbm.at[:, :, wcols(0)], cw_ref.at[:, :, wcols(0)], 2),
        load(cw_hbm.at[:, :, wcols(1)], cw_ref.at[:, :, wcols(1)], 3),
        load(cw_hbm.at[:, :, wcols(2)], cw_ref.at[:, :, wcols(2)], 4),
        load(cb_hbm, cb_ref, 5),
        load(ag_hbm, ag_ref, 6),
        load(wk_hbm, wkv_ref.at[:, 0:DH], 7),
        load(wv_hbm, wkv_ref.at[:, DH : 2 * DH], 8),
        load(wq_hbm, wq_ref, 9),
        load(wo_hbm, wo_ref, 10),
    ]
    for cp in loads[:7]:
        cp.start()

    barrier = pltpu.get_barrier_semaphore()
    for who in (nxt, prv, a_up, a_dn, b_up, b_dn, a_far, b_far, mate):
        pl.semaphore_signal(barrier, inc=1, device_id=(dp, who), device_id_type=MESH)

    def remote(src, dst, ss, rs, who):
        return pltpu.make_async_remote_copy(
            src_ref=src, dst_ref=dst, send_sem=ss, recv_sem=rs,
            device_id=(dp, who), device_id_type=MESH,
        )

    halo = [
        remote(x_ref.at[pl.ds(0, 8)], edge_ref.at[0], hsend.at[0], hrecv.at[0], prv),
        remote(x_ref.at[pl.ds(ROWS - 8, 8)], edge_ref.at[1], hsend.at[1], hrecv.at[1], nxt),
    ]
    def norm_rows(wide, gain):
        ms = jnp.sum(wide * wide, axis=-1, keepdims=True) * (1.0 / C)
        return wide * lax.rsqrt(ms + 1e-06) * gain

    loads[0].wait()
    loads[1].wait()
    cgain = cg_ref[...].reshape(1, C)
    for i in range(0, ROWS, 32):
        ext_ref[i : i + 32, :] = norm_rows(x_ref[i : i + 32, :].astype(F32), cgain).astype(BF)

    pl.semaphore_wait(barrier, 9)
    for cp in halo:
        cp.start()
    for cp in loads[7:]:
        cp.start()
    ring8 = lax.broadcasted_iota(jnp.int32, (8, 256), 0)
    for n in range(3):
        cols = wcols(n)
        loads[2 + n].wait()
        mid = nn_dot(ext_ref[0:ROWS, :], cw_ref[1, :, cols])
        up = pltpu.roll(nn_dot(ext_ref[0:ROWS, :], cw_ref[0, :, cols]), REACH, 0)
        dn = pltpu.roll(nn_dot(ext_ref[0:ROWS, :], cw_ref[2, :, cols]), ROWS - REACH, 0)
        up = jnp.concatenate([jnp.where(ring8 < REACH, 0.0, up[0:8]), up[8:]], axis=0)
        dn = jnp.concatenate([dn[0:-8], jnp.where(ring8 < REACH, dn[-8:], 0.0)], axis=0)
        acc_ref[:, cols] = up + mid + dn

    loads[5].wait()
    cbias = cb_ref[...].reshape(1, CO)
    for cp in halo:
        cp.wait_recv()
    last_ok = jnp.where(me < 31, 1.0, 0.0).astype(F32)
    first_ok = jnp.where(me > 0, 1.0, 0.0).astype(F32)
    edge = jnp.concatenate(
        [edge_ref[0].astype(F32) * last_ok, edge_ref[1].astype(F32) * first_ok], axis=0
    )
    edge = norm_rows(edge, cgain).astype(BF)
    for n in range(3):
        cols = wcols(n)
        up = pltpu.roll(nn_dot(edge, cw_ref[0, :, cols])[8:16], REACH, 0)
        dn = pltpu.roll(nn_dot(edge, cw_ref[2, :, cols])[0:8], REACH, 0)
        z = jnp.concatenate(
            [
                acc_ref[0:8, cols] + jnp.where(ring8 < REACH, up, 0.0),
                acc_ref[8 : ROWS - 8, cols],
                acc_ref[ROWS - 8 : ROWS, cols] + jnp.where(ring8 < REACH, 0.0, dn),
            ],
            axis=0,
        )
        g = jax.nn.gelu(z + cbias[:, cols], approximate=True)
        hid_ref[:, cols] = (x_ref[:, cols].astype(F32) + g).astype(BF)

    loads[6].wait()
    again = ag_ref[...].reshape(1, C)
    for i in range(0, ROWS, 32):
        wide = jnp.concatenate([hid_ref[i : i + 32, :], x_ref[i : i + 32, CO:]], axis=1).astype(F32)
        ain_ref[i : i + 32, :] = norm_rows(wide, again).astype(BF)

    loads[7].wait()
    loads[8].wait()
    kv = nn_dot(ain_ref[...], wkv_ref[...])
    k_ref[0] = kv[:, 0:DH].astype(BF)
    v_ref[0] = kv[:, DH : 2 * DH].T.astype(BF)

    sends = []

    def push(part, src, kind, da, db, who):
        ref = v_ref if part else k_ref
        i = len(sends)
        dst = SLOT[(kind, da, db)]
        cp = remote(ref.at[src], ref.at[dst], ssem.at[i], rsem.at[part, dst], who)
        cp.start()
        sends.append(cp)

    def forward(kind, da, db, part, legs="ABM"):
        if kind:
            return
        src = SLOT[(kind, da, db)]
        turn = -1 if part else 1
        if "A" in legs:
            if da == 0 and db == 0:
                for to, who in ((1, a_up), (3, a_dn))[::turn]:
                    push(part, src, 0, to, 0, who)
                if FAR_A:
                    push(part, src, 0, 2, 0, a_far)
            if not FAR_A and (da, db, part) == (1, 0, 0):
                push(part, src, 0, 2, 0, a_up)
            if not FAR_A and (da, db, part) == (3, 0, 1):
                push(part, src, 0, 2, 0, a_dn)
        if "B" in legs:
            if db == 0:
                for to, who in ((1, b_up), (3, b_dn))[::turn]:
                    push(part, src, 0, da, to, who)
                if da in FAR:
                    push(part, src, 0, da, 2, b_far)
            elif da not in FAR:
                if db == 1 and part == 0:
                    push(part, src, 0, da, 2, b_up)
                if db == 3 and part == 1:
                    push(part, src, 0, da, 2, b_dn)
        if "M" in legs:
            push(part, src, 1, da, db, mate)

    def arrive(kind, da, db, part):
        dst = SLOT[(kind, da, db)]
        ref = v_ref if part else k_ref
        remote(ref.at[dst], ref.at[dst], ssem.at[0], rsem.at[part, dst], mate).wait_recv()

    def act(key):
        for msg in ACTS.get(key, ()):
            arrive(*msg)
            forward(*msg)

    for part in (0, 1):
        forward(0, 0, 0, part, "AM" if LATE_B else "ABM")

    loads[9].wait()
    qa = nn_dot(ain_ref[...], wq_ref[...]) * SCALE
    for h in range(HEADS):
        q_ref[h * ROWS : (h + 1) * ROWS, :] = qa[:, h * DH : (h + 1) * DH].astype(BF)

    if LATE_B:
        for part in (0, 1):
            forward(0, 0, 0, part, "B")

    def fold8(x, op):
        return op(x.reshape(x.shape[0] // 8, 8, x.shape[1]), axis=0)

    def scores(slot, r, buf, j):
        s = nt_dot(k_ref[slot], q_ref[r * ROWS : (r + 1) * ROWS, :])
        s_ref[buf, j * 256 : (j + 1) * 256, :] = s
        return fold8(s, jnp.max)

    stat_ref[0:8, :] = jnp.full((8, HEADS * ROWS), -jnp.inf, F32)
    stat_ref[8:16, :] = jnp.zeros((8, HEADS * ROWS), F32)
    acc_ref[0:DH, :] = jnp.zeros((DH, HEADS * ROWS), F32)
    act((0, 0))
    slots = [SLOT[b] for b in CHUNKS[0]]
    top = None
    for j, sl in enumerate(slots):
        t = scores(sl, 0, 0, j)
        top = t if top is None else jnp.maximum(top, t)
    for i in range(len(CHUNKS)):
        slots = [SLOT[b] for b in CHUNKS[i]]
        for r in range(HEADS):
            if (i, r) != (0, 0):
                act((i, r))
            if r < HEADS - 1:
                ahead = [(SLOT[b], r + 1) for b in CHUNKS[i]]
            elif i + 1 < len(CHUNKS):
                ahead = [(SLOT[b], 0) for b in CHUNKS[i + 1]]
            else:
                ahead = []
            buf = (i * HEADS + r) % 2
            lanes = slice(r * ROWS, (r + 1) * ROWS)
            m_old = stat_ref[0:1, lanes]
            m_new = jnp.maximum(m_old, jnp.max(top, axis=0, keepdims=True))
            alpha = jnp.exp2(m_old - m_new)
            stat_ref[0:1, lanes] = m_new
            ntop = None
            total = None
            pv = None
            for j in range(max(len(slots), len(ahead))):
                if j < len(ahead):
                    t = scores(ahead[j][0], ahead[j][1], 1 - buf, j)
                    ntop = t if ntop is None else jnp.maximum(ntop, t)
                if j < len(slots):
                    p = jnp.exp2(s_ref[buf, j * 256 : (j + 1) * 256, :] - m_new)
                    y = fold8(p, jnp.sum)
                    total = y if total is None else total + y
                    z = nn_dot(v_ref[slots[j]], p.astype(BF))
                    pv = z if pv is None else pv + z
            stat_ref[8:16, lanes] = stat_ref[8:16, lanes] * alpha + total
            acc_ref[0:DH, lanes] = acc_ref[0:DH, lanes] * alpha + pv
            top = ntop

    for h in range(HEADS):
        lanes = slice(h * ROWS, (h + 1) * ROWS)
        o = acc_ref[0:DH, lanes] / jnp.sum(stat_ref[8:16, lanes], axis=0, keepdims=True)
        att_ref[:, h * DH : (h + 1) * DH] = o.T.astype(BF)
    loads[10].wait()
    for n in range(6):
        cols = slice(n * 256, (n + 1) * 256)
        base = hid_ref[:, cols] if n < 3 else x_ref[:, cols]
        y = base.astype(F32) + nn_dot(att_ref[...], wo_ref[:, cols])
        out_ref[:, cols] = y.astype(BF)

    for cp in halo + sends:
        cp.wait_send()


def body(x, cg, cw, cb, ag, wq, wk, wv, wo):
    any_spec = pl.BlockSpec(memory_space=pl.ANY)
    return pl.pallas_call(
        kernel,
        out_shape=jax.ShapeDtypeStruct((ROWS, C), BF),
        in_specs=[any_spec] * 9,
        out_specs=pl.BlockSpec(memory_space=pltpu.VMEM),
        scratch_shapes=[
            pltpu.VMEM((ROWS, C), BF),
            pltpu.VMEM((C,), F32),
            pltpu.VMEM((3, C, CO), BF),
            pltpu.VMEM((CO,), F32),
            pltpu.VMEM((C,), F32),
            pltpu.VMEM((C, HEADS * DH), BF),
            pltpu.VMEM((C, 2 * DH), BF),
            pltpu.VMEM((HEADS * DH, C), BF),
            pltpu.VMEM((2, 8, C), BF),
            pltpu.VMEM((ROWS, C), BF),
            pltpu.VMEM((ROWS, CO), BF),
            pltpu.VMEM((ROWS, C), BF),
            pltpu.VMEM((HEADS * ROWS, DH), BF),
            pltpu.VMEM((32, ROWS, DH), BF),
            pltpu.VMEM((32, DH, ROWS), BF),
            pltpu.VMEM((2, 256 * max(len(c) for c in CHUNKS), ROWS), F32),
            pltpu.VMEM((ROWS, HEADS * ROWS), F32),
            pltpu.VMEM((16, HEADS * ROWS), F32),
            pltpu.VMEM((ROWS, HEADS * DH), BF),
            pltpu.SemaphoreType.DMA((11,)),
            pltpu.SemaphoreType.DMA((2,)),
            pltpu.SemaphoreType.DMA((2,)),
            pltpu.SemaphoreType.DMA((62,)),
            pltpu.SemaphoreType.DMA((2, 32)),
        ],
        compiler_params=pltpu.CompilerParams(
            collective_id=0, has_side_effects=True, vmem_limit_bytes=40 << 20
        ),
        name="block",
    )(*(pltpu.with_memory_space_constraint(t, pltpu.HBM) for t in (x, cg, cw, cb, ag, wq, wk, wv, wo)))


def solution(mesh):
    placed = (P(("dp", "seq"), None), P(), P(), P(), P(), P(), P(), P(), P())
    return jax.shard_map(
        body, mesh=mesh, in_specs=placed, out_specs=P(("dp", "seq"), None), check_vma=False
    )
```

```python
import jax
import jax.numpy as jnp
from jax import lax
from jax.experimental import pallas as pl
from jax.experimental.pallas import tpu as pltpu
from jax.sharding import PartitionSpec as P

ROWS = 256
BULK = 240
C = 1536
CO = 768
HEADS = 4
DH = 128
REACH = 4
SIDE = 4
SCALE = 1.4426950408889634 / (DH**0.5)
BF = jnp.bfloat16
F32 = jnp.float32

FAR = (2,)
FAR_A = False
LATE_B = False
EDGE_AT = (3, 7, 9)
CHUNKS = (
    ((0, 0, 0), (1, 0, 0),),
    ((0, 1, 0), (0, 3, 0), (0, 0, 1),),
    ((0, 0, 3), (1, 3, 0), (1, 1, 0),),
    ((1, 0, 3), (1, 0, 1), (0, 2, 0),),
    ((0, 3, 3), (1, 2, 0), (0, 1, 3),),
    ((0, 3, 1), (1, 3, 3), (0, 1, 1),),
    ((0, 0, 2), (1, 3, 1), (1, 1, 3),),
    ((1, 1, 1), (1, 0, 2), (0, 2, 3),),
    ((0, 2, 1), (0, 3, 2), (1, 2, 3),),
    ((0, 1, 2), (0, 2, 2), (1, 2, 1),),
    ((2, 0, 0), (2, 1, 0),),
    ((1, 3, 2), (1, 1, 2), (1, 2, 2),),
)
ACTS = {
    (0, 0): ((1, 0, 0, 0), (1, 0, 0, 1),),
    (0, 3): ((0, 1, 0, 0), (0, 3, 0, 0), (0, 0, 1, 0), (0, 0, 3, 0), (0, 3, 0, 1), (0, 1, 0, 1), (0, 0, 3, 1), (0, 0, 1, 1),),
    (1, 3): ((1, 1, 0, 0), (1, 3, 0, 0), (1, 3, 0, 1), (1, 1, 0, 1),),
    (2, 3): ((0, 2, 0, 0), (0, 1, 3, 0), (0, 1, 1, 0), (0, 3, 3, 0), (1, 0, 1, 0), (1, 0, 3, 0), (1, 0, 3, 1), (1, 0, 1, 1), (0, 3, 1, 0), (0, 2, 0, 1),),
    (3, 3): ((0, 0, 2, 0), (0, 3, 3, 1), (1, 2, 0, 0), (1, 2, 0, 1), (0, 3, 1, 1), (0, 1, 3, 1),),
    (4, 3): ((0, 1, 1, 1), (0, 0, 2, 1), (1, 3, 3, 0), (1, 3, 3, 1),),
    (5, 3): ((0, 2, 1, 0), (0, 2, 3, 0), (1, 1, 3, 0), (1, 3, 1, 0), (1, 3, 1, 1), (1, 1, 3, 1),),
    (6, 3): ((0, 2, 2, 0), (0, 1, 2, 0), (0, 2, 3, 1), (1, 1, 1, 0), (1, 0, 2, 0), (1, 1, 1, 1), (1, 0, 2, 1),),
    (7, 3): ((0, 3, 2, 0), (1, 2, 3, 0), (0, 2, 1, 1), (0, 3, 2, 1), (1, 2, 3, 1),),
    (8, 3): ((0, 1, 2, 1), (0, 2, 2, 1), (1, 2, 1, 0), (1, 2, 1, 1),),
    (10, 3): ((1, 2, 2, 0), (1, 1, 2, 0), (1, 3, 2, 0), (1, 3, 2, 1), (1, 1, 2, 1), (1, 2, 2, 1),),
}


ORDER = tuple(b for ch in CHUNKS for b in ch if b[0] < 2)
SLOT = {b: i for i, b in enumerate(ORDER)}


def nt_dot(a, b):
    return lax.dot_general(a, b, (((1,), (1,)), ((), ())), preferred_element_type=F32)


def nn_dot(a, b):
    return jnp.dot(a, b, preferred_element_type=F32)


def kernel(
    x_hbm, cg_hbm, cw_hbm, cb_hbm, ag_hbm, wq_hbm, wk_hbm, wv_hbm, wo_hbm,
    out_ref,
    x_ref, cg_ref, cw_ref, cb_ref, ag_ref, wq_ref, wkv_ref, wo_ref,
    edge_ref, ext_ref, hid_ref, ain_ref, q_ref, k_ref, v_ref,
    s_ref, acc_ref, stat_ref, att_ref, qf_ref, he_ref, e_ref, ve_ref,
    lsem, hsend, hrecv, ssem, rsem, esend, erecv,
):
    dp = lax.axis_index("dp")
    me = lax.axis_index("seq")
    core = lax.rem(me, 2)
    chip = me // 2
    cx = chip // SIDE
    cy = lax.rem(chip, SIDE)

    def at(ix, iy, co):
        return (lax.rem(ix, SIDE) * SIDE + lax.rem(iy, SIDE)) * 2 + co

    da_x = 1 - core
    da_y = core
    a_up = at(cx + da_x, cy + da_y, core)
    a_dn = at(cx + da_x * 3, cy + da_y * 3, core)
    b_up = at(cx + da_y, cy + da_x, core)
    b_dn = at(cx + da_y * 3, cy + da_x * 3, core)
    a_far = at(cx + da_x * 2, cy + da_y * 2, core)
    b_far = at(cx + da_y * 2, cy + da_x * 2, core)
    mate = chip * 2 + (1 - core)
    nxt = lax.rem(me + 1, 32)
    prv = lax.rem(me + 31, 32)
    MESH = pl.DeviceIdType.MESH

    def load(src, dst, i):
        return pltpu.make_async_copy(src, dst, lsem.at[i])

    def wcols(n):
        return slice(n * 256, (n + 1) * 256)

    loads = [
        load(x_hbm, x_ref, 0),
        load(cg_hbm, cg_ref, 1),
        load(cw_hbm.at[:, :, wcols(0)], cw_ref.at[:, :, wcols(0)], 2),
        load(cw_hbm.at[:, :, wcols(1)], cw_ref.at[:, :, wcols(1)], 3),
        load(cw_hbm.at[:, :, wcols(2)], cw_ref.at[:, :, wcols(2)], 4),
        load(cb_hbm, cb_ref, 5),
        load(ag_hbm, ag_ref, 6),
        load(wk_hbm, wkv_ref.at[:, 0:DH], 7),
        load(wv_hbm, wkv_ref.at[:, DH : 2 * DH], 8),
        load(wq_hbm, wq_ref, 9),
        load(wo_hbm, wo_ref, 10),
    ]
    for cp in loads[:7]:
        cp.start()

    barrier = pltpu.get_barrier_semaphore()
    for who in (nxt, prv, a_up, a_dn, b_up, b_dn, a_far, b_far, mate):
        pl.semaphore_signal(barrier, inc=1, device_id=(dp, who), device_id_type=MESH)

    def remote(src, dst, ss, rs, who):
        return pltpu.make_async_remote_copy(
            src_ref=src, dst_ref=dst, send_sem=ss, recv_sem=rs,
            device_id=(dp, who), device_id_type=MESH,
        )

    halo = [
        remote(x_ref.at[pl.ds(0, 8)], edge_ref.at[0], hsend.at[0], hrecv.at[0], prv),
        remote(x_ref.at[pl.ds(ROWS - 8, 8)], edge_ref.at[1], hsend.at[1], hrecv.at[1], nxt),
    ]
    def norm_rows(wide, gain):
        ms = jnp.sum(wide * wide, axis=-1, keepdims=True) * (1.0 / C)
        return wide * lax.rsqrt(ms + 1e-06) * gain

    loads[0].wait()
    loads[1].wait()
    cgain = cg_ref[...].reshape(1, C)
    for i in range(0, ROWS, 32):
        ext_ref[i : i + 32, :] = norm_rows(x_ref[i : i + 32, :].astype(F32), cgain).astype(BF)

    pl.semaphore_wait(barrier, 9)
    for cp in halo:
        cp.start()
    for cp in loads[7:]:
        cp.start()
    ring8 = lax.broadcasted_iota(jnp.int32, (8, 256), 0)
    for n in range(3):
        cols = wcols(n)
        loads[2 + n].wait()
        mid = nn_dot(ext_ref[0:ROWS, :], cw_ref[1, :, cols])
        up = pltpu.roll(nn_dot(ext_ref[0:ROWS, :], cw_ref[0, :, cols]), REACH, 0)
        dn = pltpu.roll(nn_dot(ext_ref[0:ROWS, :], cw_ref[2, :, cols]), ROWS - REACH, 0)
        up = jnp.concatenate([jnp.where(ring8 < REACH, 0.0, up[0:8]), up[8:]], axis=0)
        dn = jnp.concatenate([dn[0:-8], jnp.where(ring8 < REACH, dn[-8:], 0.0)], axis=0)
        acc_ref[:, cols] = up + mid + dn

    loads[5].wait()
    cbias = cb_ref[...].reshape(1, CO)
    for n in range(3):
        cols = wcols(n)
        g = jax.nn.gelu(acc_ref[:, cols] + cbias[:, cols], approximate=True)
        hid_ref[:, cols] = (x_ref[:, cols].astype(F32) + g).astype(BF)

    loads[6].wait()
    again = ag_ref[...].reshape(1, C)
    for i in range(0, ROWS, 32):
        wide = jnp.concatenate([hid_ref[i : i + 32, :], x_ref[i : i + 32, CO:]], axis=1).astype(F32)
        ain_ref[i : i + 32, :] = norm_rows(wide, again).astype(BF)

    loads[7].wait()
    loads[8].wait()
    kv = nn_dot(ain_ref[...], wkv_ref[...])
    k_ref[0] = kv[8 : ROWS - 8, 0:DH].astype(BF)
    vals = jnp.concatenate([kv[8 : ROWS - 8, DH : 2 * DH], jnp.zeros((16, DH), F32)], axis=0)
    v_ref[0] = vals.T.astype(BF)

    sends = []

    def push(part, src, kind, da, db, who):
        ref = v_ref if part else k_ref
        i = len(sends)
        dst = SLOT[(kind, da, db)]
        cp = remote(ref.at[src], ref.at[dst], ssem.at[i], rsem.at[part, dst], who)
        cp.start()
        sends.append(cp)

    def forward(kind, da, db, part, legs="ABM"):
        if kind:
            return
        src = SLOT[(kind, da, db)]
        turn = -1 if part else 1
        if "A" in legs:
            if da == 0 and db == 0:
                for to, who in ((1, a_up), (3, a_dn))[::turn]:
                    push(part, src, 0, to, 0, who)
                if FAR_A:
                    push(part, src, 0, 2, 0, a_far)
            if not FAR_A and (da, db, part) == (1, 0, 0):
                push(part, src, 0, 2, 0, a_up)
            if not FAR_A and (da, db, part) == (3, 0, 1):
                push(part, src, 0, 2, 0, a_dn)
        if "B" in legs:
            if db == 0:
                for to, who in ((1, b_up), (3, b_dn))[::turn]:
                    push(part, src, 0, da, to, who)
                if da in FAR:
                    push(part, src, 0, da, 2, b_far)
            elif da not in FAR:
                if db == 1 and part == 0:
                    push(part, src, 0, da, 2, b_up)
                if db == 3 and part == 1:
                    push(part, src, 0, da, 2, b_dn)
        if "M" in legs:
            push(part, src, 1, da, db, mate)

    def arrive(kind, da, db, part):
        dst = SLOT[(kind, da, db)]
        ref = v_ref if part else k_ref
        remote(ref.at[dst], ref.at[dst], ssem.at[0], rsem.at[part, dst], mate).wait_recv()

    def act(key):
        for msg in ACTS.get(key, ()):
            arrive(*msg)
            forward(*msg)

    for part in (0, 1):
        forward(0, 0, 0, part, "AM" if LATE_B else "ABM")

    loads[9].wait()
    qf_ref[...] = nn_dot(ain_ref[...], wq_ref[...]) * SCALE

    if LATE_B:
        for part in (0, 1):
            forward(0, 0, 0, part, "B")

    for cp in halo:
        cp.wait_recv()
    last_ok = jnp.where(me < 31, 1.0, 0.0).astype(F32)
    first_ok = jnp.where(me > 0, 1.0, 0.0).astype(F32)
    edge = jnp.concatenate(
        [edge_ref[0].astype(F32) * last_ok, edge_ref[1].astype(F32) * first_ok], axis=0
    )
    edge = norm_rows(edge, cgain).astype(BF)

    def ends(v):
        return jnp.concatenate([v[0:8], v[-8:]], axis=0)

    x_ends = ends(jnp.concatenate([x_ref[0:16, :], x_ref[ROWS - 16 : ROWS, :]], axis=0).astype(F32))
    for n in range(3):
        cols = wcols(n)
        up = pltpu.roll(nn_dot(edge, cw_ref[0, :, cols])[8:16], REACH, 0)
        dn = pltpu.roll(nn_dot(edge, cw_ref[2, :, cols])[0:8], REACH, 0)
        z = jnp.concatenate(
            [
                acc_ref[0:8, cols] + jnp.where(ring8 < REACH, up, 0.0),
                acc_ref[ROWS - 8 : ROWS, cols] + jnp.where(ring8 < REACH, 0.0, dn),
            ],
            axis=0,
        )
        g = jax.nn.gelu(z + cbias[:, cols], approximate=True)
        he_ref[:, cols] = (x_ends[:, cols] + g).astype(BF).astype(F32)
    ain_e = norm_rows(
        jnp.concatenate([he_ref[...], x_ends[:, CO:]], axis=1), again
    ).astype(BF)
    e_ref[0, 0, 0] = nn_dot(ain_e, wkv_ref[...]).astype(BF)

    def edge_copy(i, src, dst, who):
        return remote(e_ref.at[src], e_ref.at[dst], esend.at[i], erecv.at[i], who)

    edges = [
        edge_copy(0, (0, 0, 0), (0, 0, 1), a_up),
        edge_copy(1, (0, 0, 0), (0, 0, 3), a_dn),
        edge_copy(2, (0, 0, 0), (0, 0, 2), a_far),
        edge_copy(3, (0, 0), (0, 1), b_up),
        edge_copy(4, (0, 0), (0, 3), b_dn),
        edge_copy(5, (0, 0), (0, 2), b_far),
        edge_copy(6, (0,), (1,), mate),
    ]
    for cp in edges[0:3]:
        cp.start()
    q_e = nn_dot(ain_e, wq_ref[...]) * SCALE
    for h in range(HEADS):
        lanes = slice(h * DH, (h + 1) * DH)
        full = jnp.concatenate(
            [q_e[0:8, lanes], qf_ref[8 : ROWS - 8, lanes], q_e[8:16, lanes]], axis=0
        )
        q_ref[h * ROWS : (h + 1) * ROWS, :] = full.astype(BF)

    def edge_part(kind, lanes):
        return e_ref[kind, :, :, :, lanes].reshape(256, DH)

    def edge_step(i):
        if i == EDGE_AT[0]:
            for cp in edges[0:3]:
                cp.wait_recv()
            for cp in edges[3:6]:
                cp.start()
        if i == EDGE_AT[1]:
            for cp in edges[3:6]:
                cp.wait_recv()
            edges[6].start()
            ve_ref[0] = edge_part(0, slice(DH, 2 * DH)).astype(F32).T.astype(BF)
        if i == EDGE_AT[2]:
            edges[6].wait_recv()
            ve_ref[1] = edge_part(1, slice(DH, 2 * DH)).astype(F32).T.astype(BF)

    def fold8(x, op):
        return op(x.reshape(x.shape[0] // 8, 8, x.shape[1]), axis=0)

    def scores(block, r, buf, j):
        keys = edge_part(block[1], slice(0, DH)) if block[0] == 2 else k_ref[SLOT[block]]
        s = nt_dot(keys, q_ref[r * ROWS : (r + 1) * ROWS, :])
        s_ref[buf, j * 256 : j * 256 + s.shape[0], :] = s
        return fold8(s, jnp.max)

    def values(block, p):
        p = p.astype(BF)
        if block[0] == 2:
            return nn_dot(ve_ref[block[1]], p)
        p = jnp.concatenate([p, jnp.zeros((16, ROWS), BF)], axis=0)
        return nn_dot(v_ref[SLOT[block]], p)

    def extent(block):
        return 256 if block[0] == 2 else BULK

    stat_ref[0:8, :] = jnp.full((8, HEADS * ROWS), -jnp.inf, F32)
    stat_ref[8:16, :] = jnp.zeros((8, HEADS * ROWS), F32)
    acc_ref[0:DH, :] = jnp.zeros((DH, HEADS * ROWS), F32)
    act((0, 0))
    slots = CHUNKS[0]
    top = None
    for j, sl in enumerate(slots):
        t = scores(sl, 0, 0, j)
        top = t if top is None else jnp.maximum(top, t)
    for i in range(len(CHUNKS)):
        slots = CHUNKS[i]
        for r in range(HEADS):
            if (i, r) != (0, 0):
                act((i, r))
            if r == HEADS - 1:
                edge_step(i)
            if r < HEADS - 1:
                ahead = [(b, r + 1) for b in CHUNKS[i]]
            elif i + 1 < len(CHUNKS):
                ahead = [(b, 0) for b in CHUNKS[i + 1]]
            else:
                ahead = []
            buf = (i * HEADS + r) % 2
            lanes = slice(r * ROWS, (r + 1) * ROWS)
            m_old = stat_ref[0:1, lanes]
            m_new = jnp.maximum(m_old, jnp.max(top, axis=0, keepdims=True))
            alpha = jnp.exp2(m_old - m_new)
            stat_ref[0:1, lanes] = m_new
            ntop = None
            total = None
            pv = None
            for j in range(max(len(slots), len(ahead))):
                if j < len(ahead):
                    t = scores(ahead[j][0], ahead[j][1], 1 - buf, j)
                    ntop = t if ntop is None else jnp.maximum(ntop, t)
                if j < len(slots):
                    p = jnp.exp2(s_ref[buf, j * 256 : j * 256 + extent(slots[j]), :] - m_new)
                    y = fold8(p, jnp.sum)
                    total = y if total is None else total + y
                    z = values(slots[j], p)
                    pv = z if pv is None else pv + z
            stat_ref[8:16, lanes] = stat_ref[8:16, lanes] * alpha + total
            acc_ref[0:DH, lanes] = acc_ref[0:DH, lanes] * alpha + pv
            top = ntop

    for h in range(HEADS):
        lanes = slice(h * ROWS, (h + 1) * ROWS)
        o = acc_ref[0:DH, lanes] / jnp.sum(stat_ref[8:16, lanes], axis=0, keepdims=True)
        att_ref[:, h * DH : (h + 1) * DH] = o.T.astype(BF)
    loads[10].wait()
    for n in range(6):
        cols = slice(n * 256, (n + 1) * 256)
        base = (hid_ref[:, cols] if n < 3 else x_ref[:, cols]).astype(F32)
        if n < 3:
            base = jnp.concatenate([he_ref[0:8, cols], base[8:-8], he_ref[8:16, cols]], axis=0)
        y = base + nn_dot(att_ref[...], wo_ref[:, cols])
        out_ref[:, cols] = y.astype(BF)

    for cp in halo + sends + edges:
        cp.wait_send()


def body(x, cg, cw, cb, ag, wq, wk, wv, wo):
    any_spec = pl.BlockSpec(memory_space=pl.ANY)
    return pl.pallas_call(
        kernel,
        out_shape=jax.ShapeDtypeStruct((ROWS, C), BF),
        in_specs=[any_spec] * 9,
        out_specs=pl.BlockSpec(memory_space=pltpu.VMEM),
        scratch_shapes=[
            pltpu.VMEM((ROWS, C), BF),
            pltpu.VMEM((C,), F32),
            pltpu.VMEM((3, C, CO), BF),
            pltpu.VMEM((CO,), F32),
            pltpu.VMEM((C,), F32),
            pltpu.VMEM((C, HEADS * DH), BF),
            pltpu.VMEM((C, 2 * DH), BF),
            pltpu.VMEM((HEADS * DH, C), BF),
            pltpu.VMEM((2, 8, C), BF),
            pltpu.VMEM((ROWS, C), BF),
            pltpu.VMEM((ROWS, CO), BF),
            pltpu.VMEM((ROWS, C), BF),
            pltpu.VMEM((HEADS * ROWS, DH), BF),
            pltpu.VMEM((32, BULK, DH), BF),
            pltpu.VMEM((32, DH, ROWS), BF),
            pltpu.VMEM((2, 256 * max(len(c) for c in CHUNKS), ROWS), F32),
            pltpu.VMEM((ROWS, HEADS * ROWS), F32),
            pltpu.VMEM((16, HEADS * ROWS), F32),
            pltpu.VMEM((ROWS, HEADS * DH), BF),
            pltpu.VMEM((ROWS, HEADS * DH), F32),
            pltpu.VMEM((16, CO), F32),
            pltpu.VMEM((2, 4, 4, 16, 2 * DH), BF),
            pltpu.VMEM((2, DH, 256), BF),
            pltpu.SemaphoreType.DMA((11,)),
            pltpu.SemaphoreType.DMA((2,)),
            pltpu.SemaphoreType.DMA((2,)),
            pltpu.SemaphoreType.DMA((62,)),
            pltpu.SemaphoreType.DMA((2, 32)),
            pltpu.SemaphoreType.DMA((7,)),
            pltpu.SemaphoreType.DMA((7,)),
        ],
        compiler_params=pltpu.CompilerParams(
            collective_id=0, has_side_effects=True, vmem_limit_bytes=40 << 20
        ),
        name="block",
    )(*(pltpu.with_memory_space_constraint(t, pltpu.HBM) for t in (x, cg, cw, cb, ag, wq, wk, wv, wo)))


def solution(mesh):
    placed = (P(("dp", "seq"), None), P(), P(), P(), P(), P(), P(), P(), P())
    return jax.shard_map(
        body, mesh=mesh, in_specs=placed, out_specs=P(("dp", "seq"), None), check_vma=False
    )
```

```python
import jax
import jax.numpy as jnp
from jax import lax
from jax.experimental import pallas as pl
from jax.experimental.pallas import tpu as pltpu
from jax.sharding import PartitionSpec as P

ROWS = 256
BULK = 240
C = 1536
CO = 768
HEADS = 4
DH = 128
REACH = 4
SIDE = 4
SCALE = 1.4426950408889634 / (DH**0.5)
BF = jnp.bfloat16
F32 = jnp.float32

FAR = (2,)
FAR_A = False
LATE_B = True
EDGE_AT = (3, 7, 9)
CHUNKS = (
    ((0, 0, 0), (1, 0, 0),),
    ((0, 1, 0), (0, 3, 0), (0, 0, 1),),
    ((0, 0, 3), (1, 3, 0), (1, 1, 0),),
    ((1, 0, 3), (1, 0, 1), (0, 2, 0),),
    ((0, 3, 3), (1, 2, 0), (0, 1, 3),),
    ((0, 3, 1), (1, 3, 3), (0, 1, 1),),
    ((0, 0, 2), (1, 3, 1), (1, 1, 3),),
    ((1, 1, 1), (1, 0, 2), (0, 2, 3),),
    ((0, 2, 1), (0, 3, 2), (1, 2, 3),),
    ((0, 1, 2), (0, 2, 2), (1, 2, 1),),
    ((2, 0, 0), (2, 1, 0),),
    ((1, 3, 2), (1, 1, 2), (1, 2, 2),),
)
ACTS = {
    (0, 0): ((1, 0, 0, 0), (1, 0, 0, 1),),
    (0, 3): ((0, 1, 0, 0), (0, 3, 0, 0), (0, 0, 1, 0),),
    (1, 0): ((0, 0, 3, 0), (0, 3, 0, 1), (0, 1, 0, 1), (0, 0, 3, 1), (0, 0, 1, 1),),
    (1, 3): ((1, 1, 0, 0), (1, 3, 0, 0),),
    (2, 0): ((0, 2, 0, 0), (0, 1, 3, 0), (1, 3, 0, 1), (1, 1, 0, 1),),
    (2, 3): ((0, 1, 1, 0), (0, 3, 3, 0), (1, 0, 1, 0), (1, 0, 3, 0),),
    (3, 0): ((1, 0, 3, 1), (1, 0, 1, 1), (0, 3, 1, 0), (0, 2, 0, 1),),
    (3, 3): ((0, 0, 2, 0), (0, 3, 3, 1), (1, 2, 0, 0),),
    (4, 0): ((1, 2, 0, 1), (0, 3, 1, 1), (0, 1, 3, 1),),
    (4, 3): ((0, 1, 1, 1), (0, 0, 2, 1), (1, 3, 3, 0),),
    (5, 0): ((1, 3, 3, 1),),
    (5, 3): ((0, 2, 1, 0), (0, 2, 3, 0), (1, 1, 3, 0), (1, 3, 1, 0),),
    (6, 0): ((0, 2, 2, 0), (1, 3, 1, 1), (1, 1, 3, 1),),
    (6, 3): ((0, 1, 2, 0), (0, 2, 3, 1), (1, 1, 1, 0), (1, 0, 2, 0),),
    (7, 0): ((0, 3, 2, 0), (1, 1, 1, 1), (1, 0, 2, 1),),
    (7, 3): ((0, 2, 1, 1), (0, 3, 2, 1), (1, 2, 3, 0),),
    (8, 0): ((1, 2, 3, 1),),
    (8, 3): ((0, 1, 2, 1), (0, 2, 2, 1), (1, 2, 1, 0),),
    (9, 0): ((1, 2, 1, 1),),
    (10, 3): ((1, 2, 2, 0), (1, 1, 2, 0), (1, 3, 2, 0),),
    (11, 0): ((1, 3, 2, 1), (1, 1, 2, 1), (1, 2, 2, 1),),
}


ORDER = tuple(b for ch in CHUNKS for b in ch if b[0] < 2)
SLOT = {b: i for i, b in enumerate(ORDER)}


def nt_dot(a, b):
    return lax.dot_general(a, b, (((1,), (1,)), ((), ())), preferred_element_type=F32)


def nn_dot(a, b):
    return jnp.dot(a, b, preferred_element_type=F32)


def kernel(
    x_hbm, cg_hbm, cw_hbm, cb_hbm, ag_hbm, wq_hbm, wk_hbm, wv_hbm, wo_hbm,
    out_ref,
    x_ref, cg_ref, cw_ref, cb_ref, ag_ref, wq_ref, wkv_ref, wo_ref,
    edge_ref, ext_ref, hid_ref, ain_ref, q_ref, k_ref, v_ref,
    s_ref, acc_ref, stat_ref, att_ref, qf_ref, he_ref, e_ref, ve_ref,
    lsem, hsend, hrecv, ssem, rsem, esend, erecv,
):
    dp = lax.axis_index("dp")
    me = lax.axis_index("seq")
    core = lax.rem(me, 2)
    chip = me // 2
    cx = chip // SIDE
    cy = lax.rem(chip, SIDE)

    def at(ix, iy, co):
        return (lax.rem(ix, SIDE) * SIDE + lax.rem(iy, SIDE)) * 2 + co

    da_x = 1 - core
    da_y = core
    a_up = at(cx + da_x, cy + da_y, core)
    a_dn = at(cx + da_x * 3, cy + da_y * 3, core)
    b_up = at(cx + da_y, cy + da_x, core)
    b_dn = at(cx + da_y * 3, cy + da_x * 3, core)
    a_far = at(cx + da_x * 2, cy + da_y * 2, core)
    b_far = at(cx + da_y * 2, cy + da_x * 2, core)
    mate = chip * 2 + (1 - core)
    nxt = lax.rem(me + 1, 32)
    prv = lax.rem(me + 31, 32)
    MESH = pl.DeviceIdType.MESH

    def load(src, dst, i):
        return pltpu.make_async_copy(src, dst, lsem.at[i])

    def wcols(n):
        return slice(n * 256, (n + 1) * 256)

    loads = [
        load(x_hbm, x_ref, 0),
        load(cg_hbm, cg_ref, 1),
        load(cw_hbm.at[:, :, wcols(0)], cw_ref.at[:, :, wcols(0)], 2),
        load(cw_hbm.at[:, :, wcols(1)], cw_ref.at[:, :, wcols(1)], 3),
        load(cw_hbm.at[:, :, wcols(2)], cw_ref.at[:, :, wcols(2)], 4),
        load(cb_hbm, cb_ref, 5),
        load(ag_hbm, ag_ref, 6),
        load(wk_hbm, wkv_ref.at[:, 0:DH], 7),
        load(wv_hbm, wkv_ref.at[:, DH : 2 * DH], 8),
        load(wq_hbm, wq_ref, 9),
        load(wo_hbm, wo_ref, 10),
    ]
    for cp in loads[:7]:
        cp.start()

    barrier = pltpu.get_barrier_semaphore()
    for who in (nxt, prv, a_up, a_dn, b_up, b_dn, a_far, b_far, mate):
        pl.semaphore_signal(barrier, inc=1, device_id=(dp, who), device_id_type=MESH)

    def remote(src, dst, ss, rs, who):
        return pltpu.make_async_remote_copy(
            src_ref=src, dst_ref=dst, send_sem=ss, recv_sem=rs,
            device_id=(dp, who), device_id_type=MESH,
        )

    halo = [
        remote(x_ref.at[pl.ds(0, 8)], edge_ref.at[0], hsend.at[0], hrecv.at[0], prv),
        remote(x_ref.at[pl.ds(ROWS - 8, 8)], edge_ref.at[1], hsend.at[1], hrecv.at[1], nxt),
    ]
    def norm_rows(wide, gain):
        ms = jnp.sum(wide * wide, axis=-1, keepdims=True) * (1.0 / C)
        return wide * lax.rsqrt(ms + 1e-06) * gain

    loads[0].wait()
    loads[1].wait()
    cgain = cg_ref[...].reshape(1, C)
    for i in range(0, ROWS, 32):
        ext_ref[i : i + 32, :] = norm_rows(x_ref[i : i + 32, :].astype(F32), cgain).astype(BF)

    pl.semaphore_wait(barrier, 9)
    for cp in halo:
        cp.start()
    for cp in loads[7:]:
        cp.start()
    ring8 = lax.broadcasted_iota(jnp.int32, (8, 256), 0)
    for n in range(3):
        cols = wcols(n)
        loads[2 + n].wait()
        mid = nn_dot(ext_ref[0:ROWS, :], cw_ref[1, :, cols])
        up = pltpu.roll(nn_dot(ext_ref[0:ROWS, :], cw_ref[0, :, cols]), REACH, 0)
        dn = pltpu.roll(nn_dot(ext_ref[0:ROWS, :], cw_ref[2, :, cols]), ROWS - REACH, 0)
        up = jnp.concatenate([jnp.where(ring8 < REACH, 0.0, up[0:8]), up[8:]], axis=0)
        dn = jnp.concatenate([dn[0:-8], jnp.where(ring8 < REACH, dn[-8:], 0.0)], axis=0)
        acc_ref[:, cols] = up + mid + dn

    loads[5].wait()
    cbias = cb_ref[...].reshape(1, CO)
    for n in range(3):
        cols = wcols(n)
        g = jax.nn.gelu(acc_ref[:, cols] + cbias[:, cols], approximate=True)
        hid_ref[:, cols] = (x_ref[:, cols].astype(F32) + g).astype(BF)

    loads[6].wait()
    again = ag_ref[...].reshape(1, C)
    for i in range(0, ROWS, 32):
        wide = jnp.concatenate([hid_ref[i : i + 32, :], x_ref[i : i + 32, CO:]], axis=1).astype(F32)
        ain_ref[i : i + 32, :] = norm_rows(wide, again).astype(BF)

    loads[7].wait()
    loads[8].wait()
    kv = nn_dot(ain_ref[...], wkv_ref[...])
    k_ref[0] = kv[8 : ROWS - 8, 0:DH].astype(BF)
    vals = jnp.concatenate([kv[8 : ROWS - 8, DH : 2 * DH], jnp.zeros((16, DH), F32)], axis=0)
    v_ref[0] = vals.T.astype(BF)

    sends = []

    def push(part, src, kind, da, db, who):
        ref = v_ref if part else k_ref
        i = len(sends)
        dst = SLOT[(kind, da, db)]
        cp = remote(ref.at[src], ref.at[dst], ssem.at[i], rsem.at[part, dst], who)
        cp.start()
        sends.append(cp)

    def forward(kind, da, db, part, legs="ABM"):
        if kind:
            return
        src = SLOT[(kind, da, db)]
        turn = -1 if part else 1
        if "A" in legs:
            if da == 0 and db == 0:
                for to, who in ((1, a_up), (3, a_dn))[::turn]:
                    push(part, src, 0, to, 0, who)
                if FAR_A:
                    push(part, src, 0, 2, 0, a_far)
            if not FAR_A and (da, db, part) == (1, 0, 0):
                push(part, src, 0, 2, 0, a_up)
            if not FAR_A and (da, db, part) == (3, 0, 1):
                push(part, src, 0, 2, 0, a_dn)
        if "B" in legs:
            if db == 0:
                for to, who in ((1, b_up), (3, b_dn))[::turn]:
                    push(part, src, 0, da, to, who)
                if da in FAR:
                    push(part, src, 0, da, 2, b_far)
            elif da not in FAR:
                if db == 1 and part == 0:
                    push(part, src, 0, da, 2, b_up)
                if db == 3 and part == 1:
                    push(part, src, 0, da, 2, b_dn)
        if "M" in legs:
            push(part, src, 1, da, db, mate)

    def arrive(kind, da, db, part):
        dst = SLOT[(kind, da, db)]
        ref = v_ref if part else k_ref
        remote(ref.at[dst], ref.at[dst], ssem.at[0], rsem.at[part, dst], mate).wait_recv()

    def act(key):
        for msg in ACTS.get(key, ()):
            arrive(*msg)
            forward(*msg)

    for part in (0, 1):
        forward(0, 0, 0, part, "AM" if LATE_B else "ABM")

    loads[9].wait()
    qf_ref[...] = nn_dot(ain_ref[...], wq_ref[...]) * SCALE

    if LATE_B:
        for part in (0, 1):
            forward(0, 0, 0, part, "B")

    for cp in halo:
        cp.wait_recv()
    last_ok = jnp.where(me < 31, 1.0, 0.0).astype(F32)
    first_ok = jnp.where(me > 0, 1.0, 0.0).astype(F32)
    edge = jnp.concatenate(
        [edge_ref[0].astype(F32) * last_ok, edge_ref[1].astype(F32) * first_ok], axis=0
    )
    edge = norm_rows(edge, cgain).astype(BF)

    def ends(v):
        return jnp.concatenate([v[0:8], v[-8:]], axis=0)

    x_ends = ends(jnp.concatenate([x_ref[0:16, :], x_ref[ROWS - 16 : ROWS, :]], axis=0).astype(F32))
    for n in range(3):
        cols = wcols(n)
        up = pltpu.roll(nn_dot(edge, cw_ref[0, :, cols])[8:16], REACH, 0)
        dn = pltpu.roll(nn_dot(edge, cw_ref[2, :, cols])[0:8], REACH, 0)
        z = jnp.concatenate(
            [
                acc_ref[0:8, cols] + jnp.where(ring8 < REACH, up, 0.0),
                acc_ref[ROWS - 8 : ROWS, cols] + jnp.where(ring8 < REACH, 0.0, dn),
            ],
            axis=0,
        )
        g = jax.nn.gelu(z + cbias[:, cols], approximate=True)
        he_ref[:, cols] = (x_ends[:, cols] + g).astype(BF).astype(F32)
    ain_e = norm_rows(
        jnp.concatenate([he_ref[...], x_ends[:, CO:]], axis=1), again
    ).astype(BF)
    e_ref[0, 0, 0] = nn_dot(ain_e, wkv_ref[...]).astype(BF)

    def edge_copy(i, src, dst, who):
        return remote(e_ref.at[src], e_ref.at[dst], esend.at[i], erecv.at[i], who)

    edges = [
        edge_copy(0, (0, 0, 0), (0, 0, 1), a_up),
        edge_copy(1, (0, 0, 0), (0, 0, 3), a_dn),
        edge_copy(2, (0, 0, 0), (0, 0, 2), a_far),
        edge_copy(3, (0, 0), (0, 1), b_up),
        edge_copy(4, (0, 0), (0, 3), b_dn),
        edge_copy(5, (0, 0), (0, 2), b_far),
        edge_copy(6, (0,), (1,), mate),
    ]
    for cp in edges[0:3]:
        cp.start()
    q_e = nn_dot(ain_e, wq_ref[...]) * SCALE
    for h in range(HEADS):
        lanes = slice(h * DH, (h + 1) * DH)
        full = jnp.concatenate(
            [q_e[0:8, lanes], qf_ref[8 : ROWS - 8, lanes], q_e[8:16, lanes]], axis=0
        )
        q_ref[h * ROWS : (h + 1) * ROWS, :] = full.astype(BF)

    def edge_part(kind, lanes):
        return e_ref[kind, :, :, :, lanes].reshape(256, DH)

    def edge_step(i):
        if i == EDGE_AT[0]:
            for cp in edges[0:3]:
                cp.wait_recv()
            for cp in edges[3:6]:
                cp.start()
        if i == EDGE_AT[1]:
            for cp in edges[3:6]:
                cp.wait_recv()
            edges[6].start()
            ve_ref[0] = edge_part(0, slice(DH, 2 * DH)).astype(F32).T.astype(BF)
        if i == EDGE_AT[2]:
            edges[6].wait_recv()
            ve_ref[1] = edge_part(1, slice(DH, 2 * DH)).astype(F32).T.astype(BF)

    def fold8(x, op):
        return op(x.reshape(x.shape[0] // 8, 8, x.shape[1]), axis=0)

    def scores(block, r, buf, j):
        keys = edge_part(block[1], slice(0, DH)) if block[0] == 2 else k_ref[SLOT[block]]
        s = nt_dot(keys, q_ref[r * ROWS : (r + 1) * ROWS, :])
        s_ref[buf, j * 256 : j * 256 + s.shape[0], :] = s
        return fold8(s, jnp.max)

    def values(block, p):
        p = p.astype(BF)
        if block[0] == 2:
            return nn_dot(ve_ref[block[1]], p)
        p = jnp.concatenate([p, jnp.zeros((16, ROWS), BF)], axis=0)
        return nn_dot(v_ref[SLOT[block]], p)

    def extent(block):
        return 256 if block[0] == 2 else BULK

    stat_ref[0:8, :] = jnp.full((8, HEADS * ROWS), -jnp.inf, F32)
    stat_ref[8:16, :] = jnp.zeros((8, HEADS * ROWS), F32)
    acc_ref[0:DH, :] = jnp.zeros((DH, HEADS * ROWS), F32)
    act((0, 0))
    slots = CHUNKS[0]
    top = None
    for j, sl in enumerate(slots):
        t = scores(sl, 0, 0, j)
        top = t if top is None else jnp.maximum(top, t)
    for i in range(len(CHUNKS)):
        slots = CHUNKS[i]
        for r in range(HEADS):
            if (i, r) != (0, 0):
                act((i, r))
            if r == HEADS - 1:
                edge_step(i)
            if r < HEADS - 1:
                ahead = [(b, r + 1) for b in CHUNKS[i]]
            elif i + 1 < len(CHUNKS):
                ahead = [(b, 0) for b in CHUNKS[i + 1]]
            else:
                ahead = []
            buf = (i * HEADS + r) % 2
            lanes = slice(r * ROWS, (r + 1) * ROWS)
            m_old = stat_ref[0:1, lanes]
            m_new = jnp.maximum(m_old, jnp.max(top, axis=0, keepdims=True))
            alpha = jnp.exp2(m_old - m_new)
            stat_ref[0:1, lanes] = m_new
            ntop = None
            total = None
            pv = None
            for j in range(max(len(slots), len(ahead))):
                if j < len(ahead):
                    t = scores(ahead[j][0], ahead[j][1], 1 - buf, j)
                    ntop = t if ntop is None else jnp.maximum(ntop, t)
                if j < len(slots):
                    p = jnp.exp2(s_ref[buf, j * 256 : j * 256 + extent(slots[j]), :] - m_new)
                    y = fold8(p, jnp.sum)
                    total = y if total is None else total + y
                    z = values(slots[j], p)
                    pv = z if pv is None else pv + z
            stat_ref[8:16, lanes] = stat_ref[8:16, lanes] * alpha + total
            acc_ref[0:DH, lanes] = acc_ref[0:DH, lanes] * alpha + pv
            top = ntop

    for h in range(HEADS):
        lanes = slice(h * ROWS, (h + 1) * ROWS)
        o = acc_ref[0:DH, lanes] / jnp.sum(stat_ref[8:16, lanes], axis=0, keepdims=True)
        att_ref[:, h * DH : (h + 1) * DH] = o.T.astype(BF)
    loads[10].wait()
    for n in range(6):
        cols = slice(n * 256, (n + 1) * 256)
        base = (hid_ref[:, cols] if n < 3 else x_ref[:, cols]).astype(F32)
        if n < 3:
            base = jnp.concatenate([he_ref[0:8, cols], base[8:-8], he_ref[8:16, cols]], axis=0)
        y = base + nn_dot(att_ref[...], wo_ref[:, cols])
        out_ref[:, cols] = y.astype(BF)

    for cp in halo + sends + edges:
        cp.wait_send()


def body(x, cg, cw, cb, ag, wq, wk, wv, wo):
    any_spec = pl.BlockSpec(memory_space=pl.ANY)
    return pl.pallas_call(
        kernel,
        out_shape=jax.ShapeDtypeStruct((ROWS, C), BF),
        in_specs=[any_spec] * 9,
        out_specs=pl.BlockSpec(memory_space=pltpu.VMEM),
        scratch_shapes=[
            pltpu.VMEM((ROWS, C), BF),
            pltpu.VMEM((C,), F32),
            pltpu.VMEM((3, C, CO), BF),
            pltpu.VMEM((CO,), F32),
            pltpu.VMEM((C,), F32),
            pltpu.VMEM((C, HEADS * DH), BF),
            pltpu.VMEM((C, 2 * DH), BF),
            pltpu.VMEM((HEADS * DH, C), BF),
            pltpu.VMEM((2, 8, C), BF),
            pltpu.VMEM((ROWS, C), BF),
            pltpu.VMEM((ROWS, CO), BF),
            pltpu.VMEM((ROWS, C), BF),
            pltpu.VMEM((HEADS * ROWS, DH), BF),
            pltpu.VMEM((32, BULK, DH), BF),
            pltpu.VMEM((32, DH, ROWS), BF),
            pltpu.VMEM((2, 256 * max(len(c) for c in CHUNKS), ROWS), F32),
            pltpu.VMEM((ROWS, HEADS * ROWS), F32),
            pltpu.VMEM((16, HEADS * ROWS), F32),
            pltpu.VMEM((ROWS, HEADS * DH), BF),
            pltpu.VMEM((ROWS, HEADS * DH), F32),
            pltpu.VMEM((16, CO), F32),
            pltpu.VMEM((2, 4, 4, 16, 2 * DH), BF),
            pltpu.VMEM((2, DH, 256), BF),
            pltpu.SemaphoreType.DMA((11,)),
            pltpu.SemaphoreType.DMA((2,)),
            pltpu.SemaphoreType.DMA((2,)),
            pltpu.SemaphoreType.DMA((62,)),
            pltpu.SemaphoreType.DMA((2, 32)),
            pltpu.SemaphoreType.DMA((7,)),
            pltpu.SemaphoreType.DMA((7,)),
        ],
        compiler_params=pltpu.CompilerParams(
            collective_id=0, has_side_effects=True, vmem_limit_bytes=40 << 20
        ),
        name="block",
    )(*(pltpu.with_memory_space_constraint(t, pltpu.HBM) for t in (x, cg, cw, cb, ag, wq, wk, wv, wo)))


def solution(mesh):
    placed = (P(("dp", "seq"), None), P(), P(), P(), P(), P(), P(), P(), P())
    return jax.shard_map(
        body, mesh=mesh, in_specs=placed, out_specs=P(("dp", "seq"), None), check_vma=False
    )
```
